768 devices in a mesh: grp: 4 (over x), blk: 192 (over z, y, core).
Axes of the slice: x: 4, y: 8, z: 12, core: 2. Of those that a mesh axis runs over, the one named last changes fastest.
Arguments:
- edge_state: bfloat16 [294912, 512], P(('grp', 'blk')), may hold values from -6 to 6
- basis: bfloat16 [18432, 16, 16], P(('grp', 'blk')), may hold values from -1.5 to 1.5
- weights: bfloat16 [3, 512, 512], replicated, may hold values from -0.25 to 0.25
- partner: int32 [2304], P(('grp', 'blk')), may hold values from 0 to 11, as said below
- cotangent: bfloat16 [294912, 512], P(('grp', 'blk')), may hold values from -6 to 6
Outputs:
- edge_out: bfloat16 [294912, 512], P(('grp', 'blk'))
- grad_state: bfloat16 [294912, 512], P(('grp', 'blk'))
- weight_grad: float32 [1536, 512], P(('grp', 'blk'))
The draws below stay inside these ranges and needn't reach their ends.
Inputs may be any that keep to these rules, and one draw needn't show every extreme that they name: partner pairs the blocks of each group: partner[partner[k]] = k within the group, and a block may be its own partner. A device pairs at most 1 of its blocks with blocks of any one other device of its group, and exactly 1 with those of one of them.
All inputs are finite; a program needn't handle non-finite values.
Results may differ from the reference program's by a relative error of at most 0.008.
Values may be sent and summed in bfloat16 or wider, within the bound.
No kernel may reach another device: no remote copies, remote signals or barrier semaphores. Data moves between devices by JAX's collectives and lax.ppermute only.
A program may use at most 32 MiB of HBM per device.

```python
import math
import jax
import jax.numpy as jnp
from jax import lax

D = 512
NBR = 16
BLOCK = 128
CAP = 1
NB = 3
EDGES = 294912
ATOMS = 18432
N_GRP = 4
N_BLK = 192


def draw_partner(key, part):

    def one_group(group_key):
        star_key, count_key, perm_key = jax.random.split(group_key, 3)
        star = jax.random.randint(star_key, (), 1, N_GRP)
        extra = jax.random.randint(count_key, (N_GRP,), 0, CAP + 1)
        masks = jnp.arange(N_GRP, dtype=jnp.int32)
        counts = jnp.where(masks == star, CAP, extra)
        counts = jnp.where(masks == 0, 0, counts)
        ends = jnp.cumsum(counts)
        starts = ends - counts
        rounds = jnp.arange(NB, dtype=jnp.int32)
        inside = (rounds[:, None] >= starts[None, :]) & (rounds[:, None] < ends[None, :])
        round_mask = jnp.sum(jnp.where(inside, masks[None, :], 0), axis=1).astype(jnp.int32)
        perm_keys = jax.random.split(perm_key, N_GRP)
        perms = jax.vmap(lambda single: jax.random.permutation(single, NB))(perm_keys).astype(jnp.int32)
        peer = jnp.bitwise_xor(masks[:, None], round_mask[None, :])
        peer_block = perms[peer, rounds[None, :]]
        value = (peer * NB + peer_block).astype(jnp.int32)
        inverse = jnp.argsort(perms, axis=1).astype(jnp.int32)
        return jnp.take_along_axis(value, inverse, axis=1)
    groups = jax.vmap(one_group)(jax.random.split(key, N_BLK))
    return jnp.swapaxes(groups, 0, 1).reshape(-1).astype(jnp.int32)


def levels(own_key, extent, pieces, smallest, largest):
    def one(dim, parts):
        draws = jax.random.uniform(jax.random.fold_in(jax.random.fold_in(own_key, 6), dim), (parts,), jnp.float32, smallest / len(pieces), largest / len(pieces))
        return jnp.repeat(jnp.exp(draws), extent[dim] // parts).reshape((-1,) + (1,) * (len(extent) - dim - 1))

    factor_of = one(*pieces[0])
    for cut in pieces[1:]:
        factor_of = factor_of * one(*cut)
    return factor_of


def gaussian(rng, dims, scale, most, cuts=(), kind=jnp.bfloat16):
    result = scale * jax.random.normal(rng, dims, jnp.float32)
    if cuts:
        result = result * levels(rng, dims, cuts, -0.22, 0.18)
    return jnp.clip(result, -most, most).astype(kind)


def setup_inputs(seed: int = 0) -> dict:
    arg_keys = jax.random.split(jax.random.key(seed), 6)
    edge_state = gaussian(arg_keys[0], (EDGES, D), 1.0, 6.0, ((0, 768),))
    basis = gaussian(arg_keys[1], (ATOMS, NBR, NBR), 0.25, 1.5, ((0, 768),))
    weights = gaussian(arg_keys[2], (3, D, D), D ** -0.5, 0.25)
    partner = draw_partner(jax.random.fold_in(arg_keys[5], 71), 0)
    cotangent = gaussian(arg_keys[4], (EDGES, D), 1.0, 6.0, ((0, 768),))
    return dict(edge_state=edge_state, basis=basis, weights=weights, partner=partner, cotangent=cotangent)


def norm_rows(hidden):
    return hidden * lax.rsqrt(lax.optimization_barrier(jnp.mean(hidden * hidden, axis=-1, keepdims=True)) + 1e-06)

def layer_forward(hidden, weight):
    normed = norm_rows(hidden).astype(jnp.bfloat16)
    preact = jnp.dot(normed, weight, preferred_element_type=jnp.float32)
    return (hidden + jax.nn.silu(preact), normed, preact)

def layer_backward(hidden, normed, preact, weight, upstream):
    sigma = jax.nn.sigmoid(preact)
    grad_pre = (upstream * sigma * (1.0 + preact * (1.0 - sigma))).astype(jnp.bfloat16)
    grad_weight = lax.dot_general(normed, grad_pre, (((0,), (0,)), ((), ())), preferred_element_type=jnp.float32)
    grad_normed = lax.dot_general(grad_pre, weight, (((1,), (1,)), ((), ())), preferred_element_type=jnp.float32)
    inverse = lax.rsqrt(lax.optimization_barrier(jnp.mean(hidden * hidden, axis=-1, keepdims=True)) + 1e-06)
    unit = hidden * inverse
    inner = lax.optimization_barrier(jnp.mean(grad_normed * unit, axis=-1, keepdims=True))
    return (upstream + inverse * (grad_normed - unit * inner), grad_weight)

def flip_rows(blocks):
    count, height, width = blocks.shape
    return blocks.reshape(count, height // 2, 2, width)[:, :, ::-1, :].reshape(count, height, width)

def reverse_group(values, group_partner):
    blocks = values.reshape(-1, BLOCK, D)
    return flip_rows(blocks[group_partner]).reshape(-1, D)

def reference(edge_state, basis, weights, partner, cotangent):
    edges_dev = NB * BLOCK
    state_grid = edge_state.reshape(N_GRP, N_BLK, edges_dev, D)
    basis_grid = basis.reshape(N_GRP, N_BLK, edges_dev // NBR, NBR, NBR)
    cot_grid = cotangent.reshape(N_GRP, N_BLK, edges_dev, D)
    partner_grid = partner.reshape(N_GRP, N_BLK, NB)

    def one_group(total, group_index):
        states = lax.dynamic_index_in_dim(state_grid, group_index, 1, keepdims=False)
        bases = lax.dynamic_index_in_dim(basis_grid, group_index, 1, keepdims=False).reshape(-1, NBR, NBR)
        upstream = lax.dynamic_index_in_dim(cot_grid, group_index, 1, keepdims=False).reshape(-1, D)
        group_partner = lax.dynamic_index_in_dim(partner_grid, group_index, 1, keepdims=False).reshape(-1)
        bases_wide = bases.astype(jnp.float32)
        mixed = jnp.einsum('aij,ajd->aid', bases_wide, states.reshape(-1, NBR, D).astype(jnp.float32)).reshape(-1, D)
        first, normed_one, pre_one = layer_forward(mixed, weights[0])
        second, normed_two, pre_two = layer_forward(first, weights[1])
        sent = second.astype(jnp.bfloat16)
        reversed_state = reverse_group(sent, group_partner)
        summed = second + reversed_state.astype(jnp.float32)
        final, normed_three, pre_three = layer_forward(summed, weights[2])
        grad_summed, grad_three = layer_backward(summed, normed_three, pre_three, weights[2], upstream.astype(jnp.float32))
        grad_reversed = grad_summed.astype(jnp.bfloat16)
        grad_sent = reverse_group(grad_reversed, group_partner)
        grad_second = grad_summed + grad_sent.astype(jnp.float32)
        grad_first, grad_two = layer_backward(first, normed_two, pre_two, weights[1], grad_second)
        grad_mixed, grad_one = layer_backward(mixed, normed_one, pre_one, weights[0], grad_first)
        grad_round = grad_mixed.astype(jnp.bfloat16).reshape(-1, NBR, D)
        grad_input = jnp.einsum('aij,aid->ajd', bases_wide, grad_round.astype(jnp.float32))
        outputs = final.astype(jnp.bfloat16).reshape(N_GRP, edges_dev, D)
        grads = grad_input.astype(jnp.bfloat16).reshape(N_GRP, edges_dev, D)
        total = total + jnp.concatenate([grad_one, grad_two, grad_three], axis=0)
        return (total, (outputs, grads))
    start = jnp.zeros((3 * D, D), jnp.float32)
    total, (outputs, grads) = lax.scan(one_group, start, jnp.arange(N_BLK))
    edge_out = jnp.swapaxes(outputs, 0, 1).reshape(EDGES, D)
    grad_state = jnp.swapaxes(grads, 0, 1).reshape(EDGES, D)
    weight_grad = total * (1.0 / math.sqrt(EDGES))
    return (edge_out, grad_state, weight_grad)
```

```python
import functools
import math

import jax
import jax.numpy as jnp
import numpy as np
from jax import lax
from jax.experimental import pallas as pl
from jax.experimental.pallas import tpu as pltpu
from jax.sharding import Mesh
from jax.sharding import PartitionSpec as P

NBR = 16
BLOCK = 128
GRP_BLK = ("grp", "blk_0", "blk_1", "blk_2")
BF16 = jnp.bfloat16
F32 = jnp.float32


def dot(a, b):
    return jnp.dot(a, b, preferred_element_type=F32)


def dot_nt(a, b):
    return lax.dot_general(a, b, (((1,), (1,)), ((), ())), preferred_element_type=F32)


def dot_tn(a, b):
    return lax.dot_general(a, b, (((0,), (0,)), ((), ())), preferred_element_type=F32)


def inverse_norm(hidden):
    return lax.rsqrt(jnp.mean(hidden * hidden, axis=-1, keepdims=True) + 1e-06)


def sigmoid(v):
    return 1.0 / (1.0 + jnp.exp(-v))


def layer_backward(unit, inverse, preact, weight, upstream):
    sigma = sigmoid(preact)
    grad_pre = (upstream * sigma * (1.0 + preact * (1.0 - sigma))).astype(BF16)
    grad_normed = dot_nt(grad_pre, weight)
    inner = jnp.mean(grad_normed * unit, axis=-1, keepdims=True)
    return upstream + inverse * (grad_normed - unit * inner), grad_pre


def basis_blocks(basis, count):
    wide_row = lax.broadcasted_iota(jnp.int32, (NBR, BLOCK), 0)
    wide_col = lax.broadcasted_iota(jnp.int32, (NBR, BLOCK), 1)
    spread = jnp.where(wide_col % NBR == wide_row, 1.0, 0.0).astype(BF16)
    tiled = dot(basis, spread)
    row = lax.broadcasted_iota(jnp.int32, (BLOCK, BLOCK), 0)
    col = lax.broadcasted_iota(jnp.int32, (BLOCK, BLOCK), 1)
    same = row // NBR == col // NBR
    return [
        jnp.where(same, tiled[n * BLOCK : (n + 1) * BLOCK], 0.0).astype(BF16) for n in range(count)
    ]


def owner_of(number, count):
    owner = jnp.int32(0)
    for edge in range(1, 4):
        owner = owner + (number >= edge * count).astype(jnp.int32)
    return owner


def fill_slots(slots_ref, blocks_ref, partner_ref, group_count, count):
    owners = [owner_of(partner_ref[n], count) for n in range(count)]
    for d in range(group_count):
        pick = jnp.int32(0)
        for n in range(1, count):
            pick = jnp.where(owners[n] == d, n, pick)
        start = pl.multiple_of(pick * BLOCK, BLOCK)
        slots_ref[d] = blocks_ref[pl.ds(start, BLOCK), :]


def reverse_blocks(arrived_ref, own_ref, partner_ref, index_ref, count):
    row = lax.broadcasted_iota(jnp.int32, (BLOCK, BLOCK), 0)
    col = lax.broadcasted_iota(jnp.int32, (BLOCK, BLOCK), 1)
    flip = jnp.where(row + 1 - 2 * (row % 2) == col, 1.0, 0.0).astype(BF16)
    picked = []
    for n in range(count):
        number = partner_ref[n]
        owner = owner_of(number, count)
        start = pl.multiple_of((number - owner * count) * BLOCK, BLOCK)
        near = own_ref[pl.ds(start, BLOCK), :].astype(BF16)
        picked.append(dot(flip, jnp.where(owner == index_ref[0], near, arrived_ref[owner])))
    return jnp.concatenate(picked, axis=0)


def forward_body(partner_ref, edge_ref, basis_ref, weight_ref, mixed_ref, pre_one_ref, pre_two_ref,
                 second_ref, slots_ref, sent_ref):
    count = edge_ref.shape[0] // BLOCK
    blocks = basis_blocks(basis_ref[...], count)
    mixed = jnp.concatenate(
        [dot(blocks[n], edge_ref[n * BLOCK : (n + 1) * BLOCK, :]) for n in range(count)], axis=0
    )
    mixed_ref[...] = mixed
    pre_one = dot((mixed * inverse_norm(mixed)).astype(BF16), weight_ref[0])
    pre_one_ref[...] = pre_one
    first = mixed + pre_one * sigmoid(pre_one)
    pre_two = dot((first * inverse_norm(first)).astype(BF16), weight_ref[1])
    pre_two_ref[...] = pre_two
    second = first + pre_two * sigmoid(pre_two)
    second_ref[...] = second
    sent_ref[...] = second.astype(BF16)
    fill_slots(slots_ref, sent_ref, partner_ref, slots_ref.shape[0], count)


def middle_body(partner_ref, index_ref, second_ref, arrived_ref, weight_ref, cotangent_ref,
                edge_out_ref, grad_summed_ref, normed_ref, grad_pre_ref, slots_ref, sent_ref):
    count = second_ref.shape[0] // BLOCK
    summed = second_ref[...] + reverse_blocks(arrived_ref, second_ref, partner_ref, index_ref, count)
    inverse = inverse_norm(summed)
    unit = summed * inverse
    normed = unit.astype(BF16)
    normed_ref[...] = normed
    preact = dot(normed, weight_ref[2])
    edge_out_ref[...] = (summed + preact * sigmoid(preact)).astype(BF16)
    grad_summed, grad_pre = layer_backward(
        unit, inverse, preact, weight_ref[2], cotangent_ref[...].astype(F32)
    )
    grad_pre_ref[...] = grad_pre
    grad_summed_ref[...] = grad_summed
    sent_ref[...] = grad_summed.astype(BF16)
    fill_slots(slots_ref, sent_ref, partner_ref, slots_ref.shape[0], count)


def layer_pieces(layer, groups, deep):
    per_layer = groups * deep // 3
    pieces = []
    done = 0
    while done < per_layer:
        number = per_layer * layer + done
        size = min(per_layer - done, deep - number % deep)
        pieces.append((number // deep, number % deep, done, size))
        done += size
    return pieces


def row_order(groups, deep, high, cores):
    order = []
    for layer in range(3):
        rows = []
        for _, _, done, size in layer_pieces(layer, groups, deep):
            y, z, i = np.meshgrid(np.arange(high), np.arange(size), np.arange(2), indexing="ij")
            rows.append((2 * cores * high * (z + done) + 2 * cores * y + i).reshape(-1))
        rows = np.concatenate(rows)
        order.append(np.concatenate([rows, rows]))
    return np.stack(order).astype(np.int32)


def permuted(normed, order, core):
    width = normed.shape[1]
    place = lax.broadcasted_iota(jnp.int32, (1, width), 1)
    source = order + 2 * jnp.where(place < width // 2, core, 1 - core)
    row = lax.broadcasted_iota(jnp.int32, (width, width), 0)
    choice = jnp.where(row == source, 1.0, 0.0).astype(BF16)
    return dot(normed, choice).astype(BF16)


def spread_rows(wide_ref, grad_weight, layer, high):
    groups, part = wide_ref.shape[1:3]
    deep = part // (2 * high)
    half = grad_weight.shape[0] // 2
    for side in range(2):
        start = side * half
        for g, z, _, size in layer_pieces(layer, groups, deep):
            for y in range(high):
                to = 2 * deep * y + 2 * z
                wide_ref[side, g, to : to + 2 * size, :] = grad_weight[start : start + 2 * size]
                start += 2 * size


def backward_body(partner_ref, index_ref, grad_summed_ref, arrived_ref, mixed_ref, pre_one_ref,
                  pre_two_ref, normed_three_ref, grad_pre_three_ref, weight_ref, basis_ref,
                  order_ref, grad_state_ref, keep_ref, send_ref, wide_ref, *, high):
    count = mixed_ref.shape[0] // BLOCK
    mixed = mixed_ref[...]
    pre_one = pre_one_ref[...]
    pre_two = pre_two_ref[...]
    grad_second = grad_summed_ref[...] + reverse_blocks(
        arrived_ref, grad_summed_ref, partner_ref, index_ref, count
    )
    first = mixed + pre_one * sigmoid(pre_one)
    inverse_two = inverse_norm(first)
    unit_two = first * inverse_two
    grad_first, grad_pre_two = layer_backward(
        unit_two, inverse_two, pre_two, weight_ref[1], grad_second
    )
    inverse_one = inverse_norm(mixed)
    unit_one = mixed * inverse_one
    grad_mixed, grad_pre_one = layer_backward(
        unit_one, inverse_one, pre_one, weight_ref[0], grad_first
    )
    grad_round = grad_mixed.astype(BF16)
    blocks = basis_blocks(basis_ref[...], count)
    for n in range(count):
        rows = slice(n * BLOCK, (n + 1) * BLOCK)
        grad_state_ref[rows, :] = dot_tn(blocks[n], grad_round[rows]).astype(BF16)
    core = index_ref[1]
    pairs = (
        (unit_one.astype(BF16), grad_pre_one),
        (unit_two.astype(BF16), grad_pre_two),
        (normed_three_ref[...], grad_pre_three_ref[...]),
    )
    for layer, (normed, grad_pre) in enumerate(pairs):
        ordered = permuted(normed, order_ref[layer : layer + 1, :], core)
        spread_rows(wide_ref, dot_tn(ordered, grad_pre), layer, high)
    keep_ref[...] = wide_ref[0].astype(BF16)
    send_ref[...] = wide_ref[1].astype(BF16)


def call(body, name, scalars, arrays, outs, scratch):
    smem = pl.BlockSpec(memory_space=pltpu.SMEM)
    vmem = pl.BlockSpec(memory_space=pltpu.VMEM)
    return pl.pallas_call(
        body,
        name=name,
        in_specs=[smem] * len(scalars) + [vmem] * len(arrays),
        out_specs=[vmem] * len(outs),
        out_shape=[jax.ShapeDtypeStruct(*o) for o in outs],
        scratch_shapes=[pltpu.VMEM(*s) for s in scratch],
    )(*scalars, *arrays)


def summed_over(pieces, axis):
    arrived = lax.all_to_all(pieces, axis, split_axis=0, concat_axis=0, tiled=True)
    return arrived.astype(F32).sum(axis=0)


def local(edge_state, basis, weights, partner, cotangent):
    rows, width = edge_state.shape
    groups, deep, high, cores = (lax.axis_size(a) for a in GRP_BLK)
    total_edges = rows * groups * deep * high * cores
    index = jnp.stack([lax.axis_index("grp"), lax.axis_index("blk_2")]).astype(jnp.int32)
    flat_basis = basis.reshape(rows, NBR)
    full = ((rows, width), F32)
    half = ((rows, width), BF16)
    slots = ((groups, BLOCK, width), BF16)
    mixed, pre_one, pre_two, second, sent = call(
        forward_body, "forward", [partner], [edge_state, flat_basis, weights],
        [full, full, full, full, slots], [half],
    )
    arrived = lax.all_to_all(sent, "grp", split_axis=0, concat_axis=0, tiled=True)
    edge_out, grad_summed, normed_three, grad_pre_three, sent_back = call(
        middle_body, "middle", [partner, index], [second, arrived, weights, cotangent],
        [half, full, half, half, slots], [half],
    )
    returned = lax.all_to_all(sent_back, "grp", split_axis=0, concat_axis=0, tiled=True)
    part = 3 * width // (groups * cores)
    pieces = (groups, part, width)
    order = jnp.asarray(row_order(groups, deep, high, cores))
    grad_state, keep, send = call(
        functools.partial(backward_body, high=high), "backward", [partner, index],
        [grad_summed, returned, mixed, pre_one, pre_two, normed_three, grad_pre_three, weights,
         flat_basis, order],
        [half, (pieces, BF16), (pieces, BF16)],
        [((2, *pieces), F32)],
    )
    other = lax.ppermute(send, "blk_2", [(0, 1), (1, 0)])
    pair = (keep.astype(F32) + other.astype(F32)).astype(BF16)
    line = summed_over(pair, "grp").astype(BF16)
    plane = summed_over(line.reshape(high, part // high, width), "blk_1").astype(BF16)
    final = summed_over(plane.reshape(deep, part // high // deep, width), "blk_0")
    return edge_out, grad_state, final * (1.0 / math.sqrt(total_edges))


def solution(mesh):
    split = Mesh(mesh.devices.reshape(mesh.shape["grp"], 12, 8, 2), GRP_BLK)
    return jax.shard_map(
        local,
        mesh=split,
        in_specs=(P(GRP_BLK, None), P(GRP_BLK, None, None), P(), P(GRP_BLK), P(GRP_BLK, None)),
        out_specs=(P(GRP_BLK, None), P(GRP_BLK, None), P(GRP_BLK, None)),
        check_vma=False,
    )
```

```python
import functools
import math

import jax
import jax.numpy as jnp
import numpy as np
from jax import lax
from jax.experimental import pallas as pl
from jax.experimental.pallas import tpu as pltpu
from jax.sharding import Mesh
from jax.sharding import PartitionSpec as P

NBR = 16
BLOCK = 128
GRP_BLK = ("grp", "blk_0", "blk_1", "blk_2")
BF16 = jnp.bfloat16
F32 = jnp.float32


def dot(a, b):
    return jnp.dot(a, b, preferred_element_type=F32)


def dot_nt(a, b):
    return lax.dot_general(a, b, (((1,), (1,)), ((), ())), preferred_element_type=F32)


def dot_tn(a, b):
    return lax.dot_general(a, b, (((0,), (0,)), ((), ())), preferred_element_type=F32)


def inverse_norm(hidden):
    return lax.rsqrt(jnp.mean(hidden * hidden, axis=-1, keepdims=True) + 1e-06)


def sigmoid(v):
    return 1.0 / (1.0 + jnp.exp(-v))


def layer_backward(unit, inverse, preact, weight, upstream):
    sigma = sigmoid(preact)
    grad_pre = (upstream * sigma * (1.0 + preact * (1.0 - sigma))).astype(BF16)
    grad_normed = dot_nt(grad_pre, weight)
    inner = jnp.mean(grad_normed * unit, axis=-1, keepdims=True)
    return upstream + inverse * (grad_normed - unit * inner), grad_pre


def basis_blocks(basis_ref, count):
    basis = basis_ref[...].reshape(count * BLOCK, NBR)
    wide_row = lax.broadcasted_iota(jnp.int32, (NBR, BLOCK), 0)
    wide_col = lax.broadcasted_iota(jnp.int32, (NBR, BLOCK), 1)
    spread = jnp.where(wide_col % NBR == wide_row, 1.0, 0.0).astype(BF16)
    tiled = dot(basis, spread)
    row = lax.broadcasted_iota(jnp.int32, (BLOCK, BLOCK), 0)
    col = lax.broadcasted_iota(jnp.int32, (BLOCK, BLOCK), 1)
    same = row // NBR == col // NBR
    return [
        jnp.where(same, tiled[n * BLOCK : (n + 1) * BLOCK], 0.0).astype(BF16) for n in range(count)
    ]


def owner_of(number, count):
    owner = jnp.int32(0)
    for edge in range(1, 4):
        owner = owner + (number >= edge * count).astype(jnp.int32)
    return owner


def fill_slots(slots_ref, blocks_ref, partner_ref, group_count, count):
    owners = [owner_of(partner_ref[n], count) for n in range(count)]
    for d in range(group_count):
        pick = jnp.int32(0)
        for n in range(1, count):
            pick = jnp.where(owners[n] == d, n, pick)
        start = pl.multiple_of(pick * BLOCK, BLOCK)
        slots_ref[d] = blocks_ref[pl.ds(start, BLOCK), :]


def reverse_blocks(arrived_ref, own_ref, partner_ref, index_ref, count):
    row = lax.broadcasted_iota(jnp.int32, (BLOCK, BLOCK), 0)
    col = lax.broadcasted_iota(jnp.int32, (BLOCK, BLOCK), 1)
    flip = jnp.where(row + 1 - 2 * (row % 2) == col, 1.0, 0.0).astype(BF16)
    picked = []
    for n in range(count):
        number = partner_ref[n]
        owner = owner_of(number, count)
        start = pl.multiple_of((number - owner * count) * BLOCK, BLOCK)
        near = own_ref[pl.ds(start, BLOCK), :].astype(BF16)
        picked.append(dot(flip, jnp.where(owner == index_ref[0], near, arrived_ref[owner])))
    return jnp.concatenate(picked, axis=0)


def forward_body(partner_ref, index_ref, edge_ref, basis_ref, weight_ref, mixed_ref, pre_one_ref, pre_two_ref,
                 second_ref, slots_ref, sent_ref):
    count = edge_ref.shape[0] // BLOCK
    blocks = basis_blocks(basis_ref, count)
    mixed = jnp.concatenate(
        [dot(blocks[n], edge_ref[n * BLOCK : (n + 1) * BLOCK, :]) for n in range(count)], axis=0
    )
    mixed_ref[...] = mixed
    pre_one = dot((mixed * inverse_norm(mixed)).astype(BF16), weight_ref[0])
    pre_one_ref[...] = pre_one
    first = mixed + pre_one * sigmoid(pre_one)
    pre_two = dot((first * inverse_norm(first)).astype(BF16), weight_ref[1])
    pre_two_ref[...] = pre_two
    second = first + pre_two * sigmoid(pre_two)
    second_ref[...] = second
    sent_ref[...] = second.astype(BF16)
    fill_slots(slots_ref, sent_ref, partner_ref, slots_ref.shape[0], count)


def middle_body(partner_ref, index_ref, second_ref, arrived_ref, weight_ref, cotangent_ref,
                edge_out_ref, grad_summed_ref, normed_ref, grad_pre_ref, slots_ref, sent_ref):
    count = second_ref.shape[0] // BLOCK
    summed = second_ref[...] + reverse_blocks(arrived_ref, second_ref, partner_ref, index_ref, count)
    inverse = inverse_norm(summed)
    unit = summed * inverse
    normed = unit.astype(BF16)
    normed_ref[...] = normed
    preact = dot(normed, weight_ref[2])
    edge_out_ref[...] = (summed + preact * sigmoid(preact)).astype(BF16)
    grad_summed, grad_pre = layer_backward(
        unit, inverse, preact, weight_ref[2], cotangent_ref[...].astype(F32)
    )
    grad_pre_ref[...] = grad_pre
    grad_summed_ref[...] = grad_summed
    sent_ref[...] = grad_summed.astype(BF16)
    fill_slots(slots_ref, sent_ref, partner_ref, slots_ref.shape[0], count)


def layer_pieces(layer, groups, deep):
    per_layer = groups * deep // 3
    pieces = []
    done = 0
    while done < per_layer:
        number = per_layer * layer + done
        size = min(per_layer - done, deep - number % deep)
        pieces.append((number // deep, number % deep, done, size))
        done += size
    return pieces


def row_order(groups, deep, high, cores):
    order = []
    for layer in range(3):
        rows = []
        for _, _, done, size in layer_pieces(layer, groups, deep):
            y, z, i = np.meshgrid(np.arange(high), np.arange(size), np.arange(2), indexing="ij")
            rows.append((2 * cores * high * (z + done) + 2 * cores * y + i).reshape(-1))
        rows = np.concatenate(rows)
        order.append(np.concatenate([rows, rows]))
    return np.stack(order).astype(np.int32)


def permuted(normed, order, core):
    width = normed.shape[1]
    place = lax.broadcasted_iota(jnp.int32, (1, width), 1)
    source = order + 2 * jnp.where(place < width // 2, core, 1 - core)
    row = lax.broadcasted_iota(jnp.int32, (width, width), 0)
    choice = jnp.where(row == source, 1.0, 0.0).astype(BF16)
    return dot(normed, choice).astype(BF16)


def spread_rows(wide_ref, grad_weight, layer, high):
    groups, part = wide_ref.shape[1:3]
    deep = part // (2 * high)
    half = grad_weight.shape[0] // 2
    for side in range(2):
        start = side * half
        for g, z, _, size in layer_pieces(layer, groups, deep):
            for y in range(high):
                to = 2 * deep * y + 2 * z
                wide_ref[side, g, to : to + 2 * size, :] = grad_weight[start : start + 2 * size]
                start += 2 * size


def backward_body(partner_ref, index_ref, grad_summed_ref, arrived_ref, mixed_ref, pre_one_ref,
                  pre_two_ref, normed_three_ref, grad_pre_three_ref, weight_ref, basis_ref,
                  order_ref, grad_state_ref, keep_ref, send_ref, wide_ref, *, high):
    count = mixed_ref.shape[0] // BLOCK
    mixed = mixed_ref[...]
    pre_one = pre_one_ref[...]
    pre_two = pre_two_ref[...]
    grad_second = grad_summed_ref[...] + reverse_blocks(
        arrived_ref, grad_summed_ref, partner_ref, index_ref, count
    )
    first = mixed + pre_one * sigmoid(pre_one)
    inverse_two = inverse_norm(first)
    unit_two = first * inverse_two
    grad_first, grad_pre_two = layer_backward(
        unit_two, inverse_two, pre_two, weight_ref[1], grad_second
    )
    inverse_one = inverse_norm(mixed)
    unit_one = mixed * inverse_one
    grad_mixed, grad_pre_one = layer_backward(
        unit_one, inverse_one, pre_one, weight_ref[0], grad_first
    )
    grad_round = grad_mixed.astype(BF16)
    blocks = basis_blocks(basis_ref, count)
    for n in range(count):
        rows = slice(n * BLOCK, (n + 1) * BLOCK)
        grad_state_ref[rows, :] = dot_tn(blocks[n], grad_round[rows]).astype(BF16)
    core = index_ref[1]
    pairs = (
        (unit_one.astype(BF16), grad_pre_one),
        (unit_two.astype(BF16), grad_pre_two),
        (normed_three_ref[...], grad_pre_three_ref[...]),
    )
    for layer, (normed, grad_pre) in enumerate(pairs):
        ordered = permuted(normed, order_ref[layer : layer + 1, :], core)
        spread_rows(wide_ref, dot_tn(ordered, grad_pre), layer, high)
    keep_ref[...] = wide_ref[0].astype(BF16)
    send_ref[...] = wide_ref[1].astype(BF16)


def near(array):
    return pltpu.with_memory_space_constraint(array, pltpu.VMEM)


def call(body, name, scalars, arrays, outs, scratch):
    smem = pl.BlockSpec(memory_space=pltpu.SMEM)
    vmem = pl.BlockSpec(memory_space=pltpu.VMEM)
    return pl.pallas_call(
        body,
        name=name,
        in_specs=[smem] * len(scalars) + [vmem] * len(arrays),
        out_specs=[vmem] * len(outs),
        out_shape=[pltpu.VMEM(*o) for o in outs],
        scratch_shapes=[pltpu.VMEM(*s) for s in scratch],
        compiler_params=pltpu.CompilerParams(vmem_limit_bytes=24 * 1024 * 1024),
    )(*scalars, *[near(array) for array in arrays])


def summed_over(pieces, axis):
    arrived = lax.all_to_all(pieces, axis, split_axis=0, concat_axis=0, tiled=True)
    return arrived.astype(F32).sum(axis=0)


def local(edge_state, basis, weights, partner, cotangent):
    rows, width = edge_state.shape
    groups, deep, high, cores = (lax.axis_size(a) for a in GRP_BLK)
    total_edges = rows * groups * deep * high * cores
    index = jnp.stack([lax.axis_index("grp"), lax.axis_index("blk_2")]).astype(jnp.int32)
    full = ((rows, width), F32)
    half = ((rows, width), BF16)
    slots = ((groups, BLOCK, width), BF16)
    mixed, pre_one, pre_two, second, sent = call(
        forward_body, "forward", [partner, index], [edge_state, basis, weights],
        [full, full, full, full, slots], [half],
    )
    arrived = lax.all_to_all(sent, "grp", split_axis=0, concat_axis=0, tiled=True)
    edge_out, grad_summed, normed_three, grad_pre_three, sent_back = call(
        middle_body, "middle", [partner, index], [second, arrived, weights, cotangent],
        [half, full, half, half, slots], [half],
    )
    returned = lax.all_to_all(sent_back, "grp", split_axis=0, concat_axis=0, tiled=True)
    part = 3 * width // (groups * cores)
    pieces = (groups, part, width)
    order = jnp.asarray(row_order(groups, deep, high, cores))
    grad_state, keep, send = call(
        functools.partial(backward_body, high=high), "backward", [partner, index],
        [grad_summed, returned, mixed, pre_one, pre_two, normed_three, grad_pre_three, weights,
         basis, order],
        [half, (pieces, BF16), (pieces, BF16)],
        [((2, *pieces), F32)],
    )
    other = lax.ppermute(send, "blk_2", [(0, 1), (1, 0)])
    pair = (keep.astype(F32) + other.astype(F32)).astype(BF16)
    line = summed_over(pair, "grp").astype(BF16)
    plane = summed_over(line.reshape(high, part // high, width), "blk_1").astype(BF16)
    final = summed_over(plane.reshape(deep, part // high // deep, width), "blk_0")
    return edge_out, grad_state, final * (1.0 / math.sqrt(total_edges))


def solution(mesh):
    split = Mesh(mesh.devices.reshape(mesh.shape["grp"], 12, 8, 2), GRP_BLK)
    return jax.shard_map(
        local,
        mesh=split,
        in_specs=(P(GRP_BLK, None), P(GRP_BLK, None, None), P(), P(GRP_BLK), P(GRP_BLK, None)),
        out_specs=(P(GRP_BLK, None), P(GRP_BLK, None), P(GRP_BLK, None)),
        check_vma=False,
    )
```

```python
import functools
import math

import jax
import jax.numpy as jnp
import numpy as np
from jax import lax
from jax.experimental import pallas as pl
from jax.experimental.pallas import tpu as pltpu
from jax.sharding import Mesh
from jax.sharding import PartitionSpec as P

NBR = 16
BLOCK = 128
GRP_BLK = ("grp", "blk_0", "blk_1", "blk_2")
BF16 = jnp.bfloat16
F32 = jnp.float32


def dot(a, b):
    return jnp.dot(a, b, preferred_element_type=F32)


def dot_nt(a, b):
    return lax.dot_general(a, b, (((1,), (1,)), ((), ())), preferred_element_type=F32)


def dot_tn(a, b):
    return lax.dot_general(a, b, (((0,), (0,)), ((), ())), preferred_element_type=F32)


def inverse_norm(hidden):
    return lax.rsqrt(jnp.mean(hidden * hidden, axis=-1, keepdims=True) + 1e-06)


def sigmoid(v):
    return 0.5 + 0.5 * jnp.tanh(0.5 * v)


def layer_backward(unit, inverse, preact, weight, upstream):
    sigma = sigmoid(preact)
    grad_pre = (upstream * sigma * (1.0 + preact * (1.0 - sigma))).astype(BF16)
    grad_normed = dot_nt(grad_pre, weight)
    inner = jnp.mean(grad_normed * unit, axis=-1, keepdims=True)
    return upstream + inverse * (grad_normed - unit * inner), grad_pre


def basis_blocks(turned, atoms):
    pairs = NBR * NBR
    rows = atoms * NBR
    row = lax.broadcasted_iota(jnp.int32, (rows, atoms), 0)
    col = lax.broadcasted_iota(jnp.int32, (rows, atoms), 1)
    repeat = jnp.where(row // NBR == col, 1.0, 0.0).astype(BF16)
    wide = dot_nt(repeat, turned)
    row = lax.broadcasted_iota(jnp.int32, (rows, pairs), 0)
    col = lax.broadcasted_iota(jnp.int32, (rows, pairs), 1)
    wide = jnp.where(row % NBR == col // NBR, wide, 0.0).astype(BF16)
    row = lax.broadcasted_iota(jnp.int32, (pairs, BLOCK), 0)
    col = lax.broadcasted_iota(jnp.int32, (pairs, BLOCK), 1)
    tiled = dot(wide, jnp.where(row % NBR == col % NBR, 1.0, 0.0).astype(BF16))
    row = lax.broadcasted_iota(jnp.int32, (rows, BLOCK), 0)
    col = lax.broadcasted_iota(jnp.int32, (rows, BLOCK), 1)
    return jnp.where((row % BLOCK) // NBR == col // NBR, tiled, 0.0).astype(BF16)


def owner_of(number, count):
    owner = jnp.int32(0)
    for edge in range(1, 4):
        owner = owner + (number >= edge * count).astype(jnp.int32)
    return owner


def fill_slots(slots_ref, blocks_ref, scalar_ref, group_count, count):
    owners = [owner_of(scalar_ref[n], count) for n in range(count)]
    for d in range(group_count):
        pick = jnp.int32(0)
        for n in range(1, count):
            pick = jnp.where(owners[n] == d, n, pick)
        start = pl.multiple_of(pick * BLOCK, BLOCK)
        slots_ref[d] = blocks_ref[pl.ds(start, BLOCK), :]


def reverse_blocks(arrived_ref, own_ref, scalar_ref, count):
    row = lax.broadcasted_iota(jnp.int32, (BLOCK, BLOCK), 0)
    col = lax.broadcasted_iota(jnp.int32, (BLOCK, BLOCK), 1)
    flip = jnp.where(row + 1 - 2 * (row % 2) == col, 1.0, 0.0).astype(BF16)
    picked = []
    for n in range(count):
        number = scalar_ref[n]
        owner = owner_of(number, count)
        start = pl.multiple_of((number - owner * count) * BLOCK, BLOCK)
        near = own_ref[pl.ds(start, BLOCK), :].astype(BF16)
        picked.append(dot(flip, jnp.where(owner == scalar_ref[count], near, arrived_ref[owner])))
    return jnp.concatenate(picked, axis=0)


def forward_body(scalar_ref, edge_hbm, turned_hbm, weight_hbm, mixed_ref, pre_one_ref, pre_two_ref,
                 second_ref, slots_ref, blocks_ref, weight_ref, edge_ref, turned_ref, sent_ref, sems):
    rows = edge_ref.shape[0]
    count = rows // BLOCK
    turned_copy = pltpu.make_async_copy(turned_hbm, turned_ref, sems.at[0])
    edge_copy = pltpu.make_async_copy(edge_hbm, edge_ref, sems.at[1])
    weight_copies = [
        pltpu.make_async_copy(weight_hbm.at[n], weight_ref.at[n], sems.at[2 + n]) for n in range(3)
    ]
    turned_copy.start()
    edge_copy.start()
    for copy in weight_copies:
        copy.start()
    turned_copy.wait()
    blocks_ref[...] = basis_blocks(turned_ref[...], rows // NBR)
    edge_copy.wait()
    mixed = jnp.concatenate(
        [
            dot(blocks_ref[n * BLOCK : (n + 1) * BLOCK, :], edge_ref[n * BLOCK : (n + 1) * BLOCK, :])
            for n in range(count)
        ],
        axis=0,
    )
    mixed_ref[...] = mixed
    normed = (mixed * inverse_norm(mixed)).astype(BF16)
    weight_copies[0].wait()
    pre_one = dot(normed, weight_ref[0])
    pre_one_ref[...] = pre_one
    first = mixed + pre_one * sigmoid(pre_one)
    normed = (first * inverse_norm(first)).astype(BF16)
    weight_copies[1].wait()
    pre_two = dot(normed, weight_ref[1])
    pre_two_ref[...] = pre_two
    second = first + pre_two * sigmoid(pre_two)
    second_ref[...] = second
    sent_ref[...] = second.astype(BF16)
    fill_slots(slots_ref, sent_ref, scalar_ref, slots_ref.shape[0], count)
    weight_copies[2].wait()


def middle_body(scalar_ref, second_ref, arrived_ref, weight_ref, cotangent_ref, edge_out_hbm,
                grad_summed_ref, normed_ref, grad_pre_ref, slots_ref, sent_ref, edge_out_ref, sems):
    count = second_ref.shape[0] // BLOCK
    summed = second_ref[...] + reverse_blocks(arrived_ref, second_ref, scalar_ref, count)
    inverse = inverse_norm(summed)
    unit = summed * inverse
    normed = unit.astype(BF16)
    normed_ref[...] = normed
    preact = dot(normed, weight_ref[2])
    edge_out_ref[...] = (summed + preact * sigmoid(preact)).astype(BF16)
    copy = pltpu.make_async_copy(edge_out_ref, edge_out_hbm, sems.at[0])
    copy.start()
    grad_summed, grad_pre = layer_backward(
        unit, inverse, preact, weight_ref[2], cotangent_ref[...].astype(F32)
    )
    grad_pre_ref[...] = grad_pre
    grad_summed_ref[...] = grad_summed
    sent_ref[...] = grad_summed.astype(BF16)
    fill_slots(slots_ref, sent_ref, scalar_ref, slots_ref.shape[0], count)
    copy.wait()


def layer_pieces(layer, groups, deep):
    per_layer = groups * deep // 3
    pieces = []
    done = 0
    while done < per_layer:
        number = per_layer * layer + done
        size = min(per_layer - done, deep - number % deep)
        pieces.append((number // deep, number % deep, done, size))
        done += size
    return pieces


def row_order(groups, deep, high, cores):
    order = []
    for layer in range(3):
        rows = []
        for _, _, done, size in layer_pieces(layer, groups, deep):
            y, z, i = np.meshgrid(np.arange(high), np.arange(size), np.arange(2), indexing="ij")
            rows.append((2 * cores * high * (z + done) + 2 * cores * y + i).reshape(-1))
        rows = np.concatenate(rows)
        order.append(np.concatenate([rows, rows]))
    return np.stack(order).astype(np.int32)


def permuted(normed, order, core):
    width = normed.shape[1]
    place = lax.broadcasted_iota(jnp.int32, (1, width), 1)
    source = order + 2 * jnp.where(place < width // 2, core, 1 - core)
    row = lax.broadcasted_iota(jnp.int32, (width, width), 0)
    choice = jnp.where(row == source, 1.0, 0.0).astype(BF16)
    return dot(normed, choice).astype(BF16)


def halves(grad_weight, keep_ref, send_ref):
    half = grad_weight.shape[0] // 2
    keep_ref[...] = grad_weight[:half].astype(BF16)
    send_ref[...] = grad_weight[half:].astype(BF16)


def backward_body(scalar_ref, grad_summed_ref, arrived_ref, mixed_ref, pre_one_ref, pre_two_ref,
                  weight_ref, blocks_ref, order_ref, normed_three_ref,
                  grad_pre_three_ref, grad_state_hbm, keep_ref, send_ref, grad_state_ref, sems):
    count = mixed_ref.shape[0] // BLOCK
    core = scalar_ref[count + 1]
    mixed = mixed_ref[...]
    pre_one = pre_one_ref[...]
    pre_two = pre_two_ref[...]
    grad_second = grad_summed_ref[...] + reverse_blocks(
        arrived_ref, grad_summed_ref, scalar_ref, count
    )
    first = mixed + pre_one * sigmoid(pre_one)
    inverse_two = inverse_norm(first)
    unit_two = first * inverse_two
    grad_first, grad_pre_two = layer_backward(
        unit_two, inverse_two, pre_two, weight_ref[1], grad_second
    )
    inverse_one = inverse_norm(mixed)
    unit_one = mixed * inverse_one
    grad_mixed, grad_pre_one = layer_backward(
        unit_one, inverse_one, pre_one, weight_ref[0], grad_first
    )
    grad_round = grad_mixed.astype(BF16)
    for n in range(count):
        rows = slice(n * BLOCK, (n + 1) * BLOCK)
        grad_state_ref[rows, :] = dot_tn(blocks_ref[rows, :], grad_round[rows]).astype(BF16)
    copy = pltpu.make_async_copy(grad_state_ref, grad_state_hbm, sems.at[0])
    copy.start()
    pairs = (
        (unit_one.astype(BF16), grad_pre_one),
        (unit_two.astype(BF16), grad_pre_two),
        (normed_three_ref[...], grad_pre_three_ref[...]),
    )
    for layer, (normed, grad_pre) in enumerate(pairs):
        ordered = permuted(normed, order_ref[layer : layer + 1, :], core)
        halves(dot_tn(ordered, grad_pre), keep_ref.at[layer], send_ref.at[layer])
    copy.wait()


def join_body(keep_ref, other_ref, pair_ref, wide_ref, *, high):
    groups, part = wide_ref.shape[:2]
    deep = part // (2 * high)
    for layer in range(3):
        rows = keep_ref[layer].astype(F32) + other_ref[layer].astype(F32)
        start = 0
        for g, z, _, size in layer_pieces(layer, groups, deep):
            for y in range(high):
                to = 2 * deep * y + 2 * z
                wide_ref[g, to : to + 2 * size, :] = rows[start : start + 2 * size]
                start += 2 * size
    pair_ref[...] = wide_ref[...].astype(BF16)


def plane_body(column_ref, plane_ref):
    total = column_ref[0].astype(F32)
    for y in range(1, column_ref.shape[0]):
        total = total + column_ref[y].astype(F32)
    deep, pair = plane_ref.shape[:2]
    for z in range(deep):
        plane_ref[z] = total[pair * z : pair * (z + 1)].astype(BF16)


def near(array):
    return pltpu.with_memory_space_constraint(array, pltpu.VMEM)


def away(array):
    return pltpu.with_memory_space_constraint(array, pltpu.HBM)


def call(body, name, scalars, far, arrays, far_outs, outs, scratch):
    smem = pl.BlockSpec(memory_space=pltpu.SMEM)
    vmem = pl.BlockSpec(memory_space=pltpu.VMEM)
    anywhere = pl.BlockSpec(memory_space=pltpu.HBM)
    return pl.pallas_call(
        body,
        name=name,
        in_specs=[smem] * len(scalars) + [anywhere] * len(far) + [vmem] * len(arrays),
        out_specs=[anywhere] * len(far_outs) + [vmem] * len(outs),
        out_shape=[jax.ShapeDtypeStruct(*o) for o in far_outs] + [pltpu.VMEM(*o) for o in outs],
        scratch_shapes=scratch,
        compiler_params=pltpu.CompilerParams(vmem_limit_bytes=24 * 1024 * 1024),
    )(*scalars, *[away(array) for array in far], *[near(array) for array in arrays])


def summed_over(pieces, axis):
    arrived = lax.all_to_all(pieces, axis, split_axis=0, concat_axis=0, tiled=True)
    return arrived.astype(F32).sum(axis=0)


def local(edge_state, basis, weights, partner, cotangent):
    rows, width = edge_state.shape
    groups, deep, high, cores = (lax.axis_size(a) for a in GRP_BLK)
    total_edges = rows * groups * deep * high * cores
    scalars = jnp.concatenate(
        [partner, jnp.stack([lax.axis_index("grp"), lax.axis_index("blk_2")]).astype(jnp.int32)]
    )
    turned = basis.transpose(1, 2, 0).reshape(NBR * NBR, rows // NBR)
    full = ((rows, width), F32)
    half = ((rows, width), BF16)
    slots = ((groups, BLOCK, width), BF16)
    mixed, pre_one, pre_two, second, sent, blocks, weights_near = call(
        forward_body, "forward", [scalars], [edge_state, turned, weights], [], [],
        [full, full, full, full, slots, ((rows, BLOCK), BF16), (weights.shape, BF16)],
        [pltpu.VMEM(*half), pltpu.VMEM(turned.shape, BF16), pltpu.VMEM(*half),
         pltpu.SemaphoreType.DMA((5,))],
    )
    arrived = lax.all_to_all(sent, "grp", split_axis=0, concat_axis=0, tiled=True)
    edge_out, grad_summed, normed_three, grad_pre_three, sent_back = call(
        middle_body, "middle", [scalars], [], [second, arrived, weights_near, cotangent],
        [half], [full, half, half, slots],
        [pltpu.VMEM(*half), pltpu.VMEM(*half), pltpu.SemaphoreType.DMA((1,))],
    )
    returned = lax.all_to_all(sent_back, "grp", split_axis=0, concat_axis=0, tiled=True)
    order = jnp.asarray(row_order(groups, deep, high, cores))
    swap = [(0, 1), (1, 0)]
    side = (width // 2, width)
    grad_state, keep, send = call(
        backward_body, "backward", [scalars], [],
        [grad_summed, returned, mixed, pre_one, pre_two, weights_near, blocks, order,
         normed_three, grad_pre_three],
        [half], [((3, *side), BF16), ((3, *side), BF16)],
        [pltpu.VMEM(*half), pltpu.SemaphoreType.DMA((1,))],
    )
    other = lax.ppermute(send, "blk_2", swap)
    part = 3 * width // (groups * cores)
    (pair,) = call(
        functools.partial(join_body, high=high), "join", [], [],
        [keep, other], [], [((groups, part, width), BF16)],
        [pltpu.VMEM((groups, part, width), F32)],
    )
    line = summed_over(pair, "grp").astype(BF16)
    column = lax.all_to_all(
        line.reshape(high, part // high, width), "blk_1", split_axis=0, concat_axis=0, tiled=True
    )
    (plane,) = call(
        plane_body, "plane", [], [], [column], [],
        [((deep, part // high // deep, width), BF16)], [],
    )
    final = summed_over(plane, "blk_0")
    return edge_out, grad_state, final * (1.0 / math.sqrt(total_edges))


def solution(mesh):
    split = Mesh(mesh.devices.reshape(mesh.shape["grp"], 12, 8, 2), GRP_BLK)
    return jax.shard_map(
        local,
        mesh=split,
        in_specs=(P(GRP_BLK, None), P(GRP_BLK, None, None), P(), P(GRP_BLK), P(GRP_BLK, None)),
        out_specs=(P(GRP_BLK, None), P(GRP_BLK, None), P(GRP_BLK, None)),
        check_vma=False,
    )
```

```python
import math

import jax
import jax.numpy as jnp
from jax import lax
from jax.experimental import pallas as pl
from jax.experimental.pallas import tpu as pltpu
from jax.sharding import Mesh
from jax.sharding import PartitionSpec as P

NBR = 16
BLOCK = 128
GRP_BLK = ("grp", "blk_0", "blk_1", "blk_2")
BF16 = jnp.bfloat16
F32 = jnp.float32


def dot(a, b):
    return jnp.dot(a, b, preferred_element_type=F32)


def dot_nt(a, b):
    return lax.dot_general(a, b, (((1,), (1,)), ((), ())), preferred_element_type=F32)


def dot_tn(a, b):
    return lax.dot_general(a, b, (((0,), (0,)), ((), ())), preferred_element_type=F32)


def inverse_norm(hidden):
    return lax.rsqrt(jnp.mean(hidden * hidden, axis=-1, keepdims=True) + 1e-06)


def sigmoid(v):
    return 0.5 + 0.5 * jnp.tanh(0.5 * v)


def silu_slope(preact, sigma):
    return sigma * (1.0 + preact * (1.0 - sigma))


def layer_backward(unit, inverse, slope, weight, upstream):
    grad_pre = (upstream * slope).astype(BF16)
    grad_normed = dot_nt(grad_pre, weight)
    inner = jnp.mean(grad_normed * unit, axis=-1, keepdims=True)
    return upstream + inverse * (grad_normed - unit * inner), grad_pre


def basis_blocks(turned, atoms):
    pairs = NBR * NBR
    rows = atoms * NBR
    row = lax.broadcasted_iota(jnp.int32, (rows, atoms), 0)
    col = lax.broadcasted_iota(jnp.int32, (rows, atoms), 1)
    repeat = jnp.where(row // NBR == col, 1.0, 0.0).astype(BF16)
    wide = dot_nt(repeat, turned)
    row = lax.broadcasted_iota(jnp.int32, (rows, pairs), 0)
    col = lax.broadcasted_iota(jnp.int32, (rows, pairs), 1)
    wide = jnp.where(row % NBR == col // NBR, wide, 0.0).astype(BF16)
    row = lax.broadcasted_iota(jnp.int32, (pairs, BLOCK), 0)
    col = lax.broadcasted_iota(jnp.int32, (pairs, BLOCK), 1)
    tiled = dot(wide, jnp.where(row % NBR == col % NBR, 1.0, 0.0).astype(BF16))
    row = lax.broadcasted_iota(jnp.int32, (rows, BLOCK), 0)
    col = lax.broadcasted_iota(jnp.int32, (rows, BLOCK), 1)
    return jnp.where((row % BLOCK) // NBR == col // NBR, tiled, 0.0).astype(BF16)


def owner_of(number, count):
    owner = jnp.int32(0)
    for edge in range(1, 4):
        owner = owner + (number >= edge * count).astype(jnp.int32)
    return owner


def fill_slots(slots_ref, blocks_ref, partner_ref, group_count, count):
    owners = [owner_of(partner_ref[n], count) for n in range(count)]
    for d in range(group_count):
        pick = jnp.int32(0)
        for n in range(1, count):
            pick = jnp.where(owners[n] == d, n, pick)
        start = pl.multiple_of(pick * BLOCK, BLOCK)
        slots_ref[d] = blocks_ref[pl.ds(start, BLOCK), :]


def reverse_blocks(arrived_ref, own_ref, partner_ref, count):
    row = lax.broadcasted_iota(jnp.int32, (BLOCK, BLOCK), 0)
    col = lax.broadcasted_iota(jnp.int32, (BLOCK, BLOCK), 1)
    flip = jnp.where(row + 1 - 2 * (row % 2) == col, 1.0, 0.0).astype(BF16)
    picked = []
    for n in range(count):
        number = partner_ref[n]
        owner = owner_of(number, count)
        start = pl.multiple_of((number - owner * count) * BLOCK, BLOCK)
        near = own_ref[pl.ds(start, BLOCK), :].astype(BF16)
        picked.append(dot(flip, jnp.where(owner == lax.axis_index("grp"), near, arrived_ref[owner])))
    return jnp.concatenate(picked, axis=0)


def forward_body(partner_hbm, edge_hbm, turned_hbm, weight_hbm, unit_one_ref, inverse_one_ref,
                 normed_one_ref, slope_one_ref, unit_two_ref, inverse_two_ref, normed_two_ref,
                 slope_two_ref, second_ref, slots_ref, blocks_ref, weight_ref, partner_near_ref,
                 edge_ref, turned_ref, sent_ref, partner_ref, sems):
    rows = edge_ref.shape[0]
    count = rows // BLOCK
    turned_copy = pltpu.make_async_copy(turned_hbm, turned_ref, sems.at[0])
    edge_copy = pltpu.make_async_copy(edge_hbm, edge_ref, sems.at[1])
    weight_copies = [
        pltpu.make_async_copy(weight_hbm.at[n], weight_ref.at[n], sems.at[2 + n]) for n in range(3)
    ]
    partner_copies = [
        pltpu.make_async_copy(partner_hbm, partner_ref, sems.at[5]),
        pltpu.make_async_copy(partner_hbm, partner_near_ref, sems.at[6]),
    ]
    turned_copy.start()
    edge_copy.start()
    for copy in weight_copies + partner_copies:
        copy.start()
    turned_copy.wait()
    blocks_ref[...] = basis_blocks(turned_ref[...], rows // NBR)
    edge_copy.wait()
    mixed = jnp.concatenate(
        [
            dot(blocks_ref[n * BLOCK : (n + 1) * BLOCK, :], edge_ref[n * BLOCK : (n + 1) * BLOCK, :])
            for n in range(count)
        ],
        axis=0,
    )
    inverse = inverse_norm(mixed)
    unit = mixed * inverse
    normed = unit.astype(BF16)
    unit_one_ref[...] = unit
    inverse_one_ref[...] = inverse
    normed_one_ref[...] = normed
    weight_copies[0].wait()
    preact = dot(normed, weight_ref[0])
    sigma = sigmoid(preact)
    slope_one_ref[...] = silu_slope(preact, sigma)
    first = mixed + preact * sigma
    inverse = inverse_norm(first)
    unit = first * inverse
    normed = unit.astype(BF16)
    unit_two_ref[...] = unit
    inverse_two_ref[...] = inverse
    normed_two_ref[...] = normed
    weight_copies[1].wait()
    preact = dot(normed, weight_ref[1])
    sigma = sigmoid(preact)
    slope_two_ref[...] = silu_slope(preact, sigma)
    second = first + preact * sigma
    second_ref[...] = second
    sent_ref[...] = second.astype(BF16)
    for copy in partner_copies:
        copy.wait()
    fill_slots(slots_ref, sent_ref, partner_ref, slots_ref.shape[0], count)
    weight_copies[2].wait()


def middle_body(partner_ref, second_ref, arrived_ref, weight_ref, cotangent_ref, edge_out_hbm,
                grad_summed_ref, normed_ref, grad_pre_ref, slots_ref, sent_ref, edge_out_ref, sems):
    count = second_ref.shape[0] // BLOCK
    summed = second_ref[...] + reverse_blocks(arrived_ref, second_ref, partner_ref, count)
    inverse = inverse_norm(summed)
    unit = summed * inverse
    normed = unit.astype(BF16)
    normed_ref[...] = normed
    preact = dot(normed, weight_ref[2])
    sigma = sigmoid(preact)
    edge_out_ref[...] = (summed + preact * sigma).astype(BF16)
    copy = pltpu.make_async_copy(edge_out_ref, edge_out_hbm, sems.at[0])
    copy.start()
    grad_summed, grad_pre = layer_backward(
        unit, inverse, silu_slope(preact, sigma), weight_ref[2], cotangent_ref[...].astype(F32)
    )
    grad_pre_ref[...] = grad_pre
    grad_summed_ref[...] = grad_summed
    sent_ref[...] = grad_summed.astype(BF16)
    fill_slots(slots_ref, sent_ref, partner_ref, slots_ref.shape[0], count)
    copy.wait()


def split_by_core(grad_weight, tall_ref, keep_ref, send_ref, core):
    tiles, height, lanes = tall_ref.shape
    for t in range(tiles):
        tall_ref[t] = grad_weight[:, t * lanes : (t + 1) * lanes]
    for to_ref, side in ((keep_ref, core), (send_ref, 1 - core)):
        for i in range(2):
            for t in range(tiles):
                rows = tall_ref[t, pl.ds(2 * side + i, height // 4, stride=4), :]
                to_ref[i, :, t * lanes : (t + 1) * lanes] = rows.astype(BF16)


def backward_body(partner_ref, grad_summed_ref, arrived_ref, unit_one_ref, inverse_one_ref,
                  normed_one_ref, slope_one_ref, unit_two_ref, inverse_two_ref, normed_two_ref,
                  slope_two_ref, weight_ref, normed_three_ref, grad_pre_three_ref, keep_ref,
                  send_ref, grad_round_ref, tall_ref):
    count = unit_one_ref.shape[0] // BLOCK
    core = lax.axis_index("blk_2")
    grad_second = grad_summed_ref[...] + reverse_blocks(
        arrived_ref, grad_summed_ref, partner_ref, count
    )
    grad_first, grad_pre_two = layer_backward(
        unit_two_ref[...], inverse_two_ref[...], slope_two_ref[...], weight_ref[1], grad_second
    )
    grad_mixed, grad_pre_one = layer_backward(
        unit_one_ref[...], inverse_one_ref[...], slope_one_ref[...], weight_ref[0], grad_first
    )
    grad_round_ref[...] = grad_mixed.astype(BF16)
    pairs = (
        (normed_one_ref[...], grad_pre_one),
        (normed_two_ref[...], grad_pre_two),
        (normed_three_ref[...], grad_pre_three_ref[...]),
    )
    for layer, (normed, grad_pre) in enumerate(pairs):
        split_by_core(
            dot_tn(normed, grad_pre), tall_ref, keep_ref.at[layer], send_ref.at[layer], core
        )


def finish_body(grad_round_ref, blocks_ref, grad_state_hbm, grad_state_ref, sems):
    for n in range(grad_round_ref.shape[0] // BLOCK):
        rows = slice(n * BLOCK, (n + 1) * BLOCK)
        grad_state_ref[rows, :] = dot_tn(blocks_ref[rows, :], grad_round_ref[rows, :]).astype(BF16)
    copy = pltpu.make_async_copy(grad_state_ref, grad_state_hbm, sems.at[0])
    copy.start()
    copy.wait()


def join_body(keep_ref, other_ref, pair_ref):
    groups, _, part = pair_ref.shape[:3]
    height = keep_ref.shape[2]
    for layer in range(3):
        for i in range(2):
            rows = (keep_ref[layer, i].astype(F32) + other_ref[layer, i].astype(F32)).astype(BF16)
            done = 0
            while done < height:
                number = height * layer + done
                g, at = number // part, number % part
                size = min(height - done, part - at)
                pair_ref[g, i, at : at + size, :] = rows[done : done + size]
                done += size


def line_body(arrived_ref, line_ref, tall_ref, wide_ref):
    high, width = line_ref.shape[0], line_ref.shape[2]
    deep = line_ref.shape[1] // 2
    total = arrived_ref[0].astype(F32)
    for g in range(1, arrived_ref.shape[0]):
        total = total + arrived_ref[g].astype(F32)
    tiles, lanes = tall_ref.shape[0], tall_ref.shape[-1]
    for t in range(tiles):
        across = slice(t * lanes, (t + 1) * lanes)
        tall_ref[t] = total[:, :, across]
        for y in range(high):
            for i in range(2):
                wide_ref[t, y, pl.ds(i, deep, stride=2), :] = tall_ref[
                    t, i, pl.ds(y, deep, stride=high), :
                ]
        line_ref[:, :, across] = wide_ref[t].astype(BF16)


def plane_body(column_ref, plane_ref):
    total = column_ref[0].astype(F32)
    for y in range(1, column_ref.shape[0]):
        total = total + column_ref[y].astype(F32)
    deep, pair = plane_ref.shape[:2]
    for z in range(deep):
        plane_ref[z] = total[pair * z : pair * (z + 1)].astype(BF16)


def near(array):
    return pltpu.with_memory_space_constraint(array, pltpu.VMEM)


def away(array):
    return pltpu.with_memory_space_constraint(array, pltpu.HBM)


def call(body, name, scalars, far, arrays, far_outs, outs, scratch):
    smem = pl.BlockSpec(memory_space=pltpu.SMEM)
    vmem = pl.BlockSpec(memory_space=pltpu.VMEM)
    anywhere = pl.BlockSpec(memory_space=pltpu.HBM)
    return pl.pallas_call(
        body,
        name=name,
        in_specs=[smem] * len(scalars) + [anywhere] * len(far) + [vmem] * len(arrays),
        out_specs=[anywhere] * len(far_outs) + [vmem] * len(outs),
        out_shape=[jax.ShapeDtypeStruct(*o) for o in far_outs] + [pltpu.VMEM(*o) for o in outs],
        scratch_shapes=scratch,
        compiler_params=pltpu.CompilerParams(vmem_limit_bytes=24 * 1024 * 1024),
    )(*scalars, *[away(array) for array in far], *[near(array) for array in arrays])


def summed_over(pieces, axis):
    arrived = lax.all_to_all(pieces, axis, split_axis=0, concat_axis=0, tiled=True)
    return arrived.astype(F32).sum(axis=0)


def local(edge_state, basis, weights, partner, cotangent):
    rows, width = edge_state.shape
    groups, deep, high, cores = (lax.axis_size(a) for a in GRP_BLK)
    total_edges = rows * groups * deep * high * cores
    turned = basis.transpose(1, 2, 0).reshape(NBR * NBR, rows // NBR)
    full = ((rows, width), F32)
    half = ((rows, width), BF16)
    slots = ((groups, BLOCK, width), BF16)
    thin = ((rows, 1), F32)
    *saved, second, sent, blocks, weights_near, partner_near = call(
        forward_body, "forward", [], [partner, edge_state, turned, weights], [], [],
        [full, thin, half, full, full, thin, half, full, full, slots, ((rows, BLOCK), BF16),
         (weights.shape, BF16), (partner.shape, jnp.int32)],
        [pltpu.VMEM(*half), pltpu.VMEM(turned.shape, BF16), pltpu.VMEM(*half),
         pltpu.SMEM(partner.shape, jnp.int32), pltpu.SemaphoreType.DMA((7,))],
    )
    arrived = lax.all_to_all(sent, "grp", split_axis=0, concat_axis=0, tiled=True)
    edge_out, grad_summed, normed_three, grad_pre_three, sent_back = call(
        middle_body, "middle", [near(partner_near)], [], [second, arrived, weights_near, cotangent],
        [half], [full, half, half, slots],
        [pltpu.VMEM(*half), pltpu.VMEM(*half), pltpu.SemaphoreType.DMA((1,))],
    )
    returned = lax.all_to_all(sent_back, "grp", split_axis=0, concat_axis=0, tiled=True)
    swap = [(0, 1), (1, 0)]
    side = (3, 2, width // (2 * cores), width)
    keep, send, grad_round = call(
        backward_body, "backward", [near(partner_near)], [],
        [grad_summed, returned, *saved, weights_near, normed_three, grad_pre_three],
        [], [(side, BF16), (side, BF16), half], [pltpu.VMEM((width // 128, width, 128), F32)],
    )
    other = lax.ppermute(send, "blk_2", swap)
    (grad_state,) = call(
        finish_body, "finish", [], [], [grad_round, blocks], [half], [],
        [pltpu.VMEM(*half), pltpu.SemaphoreType.DMA((1,))],
    )
    part = 3 * width // (groups * cores)
    (pair,) = call(
        join_body, "join", [], [], [keep, other], [], [((groups, 2, part // 2, width), BF16)], [],
    )
    across = lax.all_to_all(pair, "grp", split_axis=0, concat_axis=0, tiled=True)
    (line,) = call(
        line_body, "line", [], [], [across], [], [((high, part // high, width), BF16)],
        [pltpu.VMEM((width // 128, 2, part // 2, 128), F32),
         pltpu.VMEM((width // 128, high, part // high, 128), F32)],
    )
    column = lax.all_to_all(
        line, "blk_1", split_axis=0, concat_axis=0, tiled=True
    )
    (plane,) = call(
        plane_body, "plane", [], [], [column], [],
        [((deep, part // high // deep, width), BF16)], [],
    )
    final = summed_over(plane, "blk_0")
    return edge_out, grad_state, final * (1.0 / math.sqrt(total_edges))


def solution(mesh):
    split = Mesh(mesh.devices.reshape(mesh.shape["grp"], 12, 8, 2), GRP_BLK)
    return jax.shard_map(
        local,
        mesh=split,
        in_specs=(P(GRP_BLK, None), P(GRP_BLK, None, None), P(), P(GRP_BLK), P(GRP_BLK, None)),
        out_specs=(P(GRP_BLK, None), P(GRP_BLK, None), P(GRP_BLK, None)),
        check_vma=False,
    )
```

```python
import math

import jax
import jax.numpy as jnp
from jax import lax
from jax.experimental import pallas as pl
from jax.experimental.pallas import tpu as pltpu
from jax.sharding import Mesh
from jax.sharding import PartitionSpec as P

NBR = 16
BLOCK = 128
GRP_BLK = ("grp", "blk_0", "blk_1", "blk_2")
BF16 = jnp.bfloat16
F32 = jnp.float32


def dot(a, b):
    return jnp.dot(a, b, preferred_element_type=F32)


def dot_nt(a, b):
    return lax.dot_general(a, b, (((1,), (1,)), ((), ())), preferred_element_type=F32)


def dot_tn(a, b):
    return lax.dot_general(a, b, (((0,), (0,)), ((), ())), preferred_element_type=F32)


def inverse_norm(hidden):
    return lax.rsqrt(jnp.mean(hidden * hidden, axis=-1, keepdims=True) + 1e-06)


def sigmoid(v):
    return 0.5 + 0.5 * jnp.tanh(0.5 * v)


def silu_slope(preact, sigma):
    return sigma * (1.0 + preact * (1.0 - sigma))


def layer_backward(unit, inverse, slope, weight, upstream):
    grad_pre = (upstream * slope).astype(BF16)
    grad_normed = dot_nt(grad_pre, weight)
    inner = jnp.mean(grad_normed * unit, axis=-1, keepdims=True)
    return upstream + inverse * (grad_normed - unit * inner), grad_pre


def basis_blocks(turned, atoms):
    pairs = NBR * NBR
    rows = atoms * NBR
    row = lax.broadcasted_iota(jnp.int32, (rows, atoms), 0)
    col = lax.broadcasted_iota(jnp.int32, (rows, atoms), 1)
    repeat = jnp.where(row // NBR == col, 1.0, 0.0).astype(BF16)
    wide = dot_nt(repeat, turned)
    row = lax.broadcasted_iota(jnp.int32, (rows, pairs), 0)
    col = lax.broadcasted_iota(jnp.int32, (rows, pairs), 1)
    wide = jnp.where(row % NBR == col // NBR, wide, 0.0).astype(BF16)
    row = lax.broadcasted_iota(jnp.int32, (pairs, BLOCK), 0)
    col = lax.broadcasted_iota(jnp.int32, (pairs, BLOCK), 1)
    tiled = dot(wide, jnp.where(row % NBR == col % NBR, 1.0, 0.0).astype(BF16))
    row = lax.broadcasted_iota(jnp.int32, (rows, BLOCK), 0)
    col = lax.broadcasted_iota(jnp.int32, (rows, BLOCK), 1)
    return jnp.where((row % BLOCK) // NBR == col // NBR, tiled, 0.0).astype(BF16)


def owner_of(number, count):
    owner = jnp.int32(0)
    for edge in range(1, 4):
        owner = owner + (number >= edge * count).astype(jnp.int32)
    return owner


def fill_slots(slots_ref, sources, partner_ref, count):
    owners = [owner_of(partner_ref[n], count) for n in range(count)]
    for d in range(slots_ref.shape[0]):
        pick = jnp.int32(0)
        for n in range(1, count):
            pick = jnp.where(owners[n] == d, n, pick)
        start = pl.multiple_of(pick * BLOCK, BLOCK)
        for at, source_ref in enumerate(sources):
            slots_ref[d, at * BLOCK : (at + 1) * BLOCK, :] = source_ref[pl.ds(start, BLOCK), :]


def reversed_blocks(arrived_ref, sources, partner_ref, count):
    row = lax.broadcasted_iota(jnp.int32, (BLOCK, BLOCK), 0)
    col = lax.broadcasted_iota(jnp.int32, (BLOCK, BLOCK), 1)
    flip = jnp.where(row + 1 - 2 * (row % 2) == col, 1.0, 0.0).astype(BF16)
    own = lax.axis_index("grp")
    picked = [[] for _ in sources]
    for n in range(count):
        number = partner_ref[n]
        owner = owner_of(number, count)
        start = pl.multiple_of((number - owner * count) * BLOCK, BLOCK)
        for at, source_ref in enumerate(sources):
            near = source_ref[pl.ds(start, BLOCK), :].astype(BF16)
            far = arrived_ref[owner, at * BLOCK : (at + 1) * BLOCK, :]
            picked[at].append(dot(flip, jnp.where(owner == own, near, far)))
    return [jnp.concatenate(blocks, axis=0) for blocks in picked]


def forward_body(partner_hbm, edge_hbm, turned_hbm, weight_hbm, cotangent_hbm, unit_one_ref, inverse_one_ref,
                 normed_one_ref, slope_one_ref, unit_two_ref, inverse_two_ref, normed_two_ref,
                 slope_two_ref, second_ref, slots_ref, blocks_ref, weight_ref, partner_near_ref,
                 cotangent_ref,
                 edge_ref, turned_ref, sent_ref, partner_ref, sems):
    rows = edge_ref.shape[0]
    count = rows // BLOCK
    turned_copy = pltpu.make_async_copy(turned_hbm, turned_ref, sems.at[0])
    edge_copy = pltpu.make_async_copy(edge_hbm, edge_ref, sems.at[1])
    weight_copies = [
        pltpu.make_async_copy(weight_hbm.at[n], weight_ref.at[n], sems.at[2 + n]) for n in range(3)
    ]
    partner_copies = [
        pltpu.make_async_copy(partner_hbm, partner_ref, sems.at[5]),
        pltpu.make_async_copy(partner_hbm, partner_near_ref, sems.at[6]),
        pltpu.make_async_copy(cotangent_hbm, cotangent_ref, sems.at[7]),
    ]
    turned_copy.start()
    edge_copy.start()
    for copy in weight_copies + partner_copies:
        copy.start()
    turned_copy.wait()
    blocks_ref[...] = basis_blocks(turned_ref[...], rows // NBR)
    edge_copy.wait()
    mixed = jnp.concatenate(
        [
            dot(blocks_ref[n * BLOCK : (n + 1) * BLOCK, :], edge_ref[n * BLOCK : (n + 1) * BLOCK, :])
            for n in range(count)
        ],
        axis=0,
    )
    inverse = inverse_norm(mixed)
    unit = mixed * inverse
    normed = unit.astype(BF16)
    unit_one_ref[...] = unit
    inverse_one_ref[...] = inverse
    normed_one_ref[...] = normed
    weight_copies[0].wait()
    preact = dot(normed, weight_ref[0])
    sigma = sigmoid(preact)
    slope_one_ref[...] = silu_slope(preact, sigma)
    first = mixed + preact * sigma
    inverse = inverse_norm(first)
    unit = first * inverse
    normed = unit.astype(BF16)
    unit_two_ref[...] = unit
    inverse_two_ref[...] = inverse
    normed_two_ref[...] = normed
    weight_copies[1].wait()
    preact = dot(normed, weight_ref[1])
    sigma = sigmoid(preact)
    slope_two_ref[...] = silu_slope(preact, sigma)
    second = first + preact * sigma
    second_ref[...] = second
    sent_ref[...] = second.astype(BF16)
    for copy in partner_copies:
        copy.wait()
    fill_slots(slots_ref, (sent_ref, cotangent_ref), partner_ref, count)
    weight_copies[2].wait()


def split_by_core(grad_weight, tall_ref, keep_ref, send_ref, core):
    tiles, height, lanes = tall_ref.shape
    for t in range(tiles):
        tall_ref[t] = grad_weight[:, t * lanes : (t + 1) * lanes]
    for to_ref, side in ((keep_ref, core), (send_ref, 1 - core)):
        for i in range(2):
            for t in range(tiles):
                rows = tall_ref[t, pl.ds(2 * side + i, height // 4, stride=4), :]
                to_ref[i, :, t * lanes : (t + 1) * lanes] = rows.astype(BF16)


def backward_body(partner_ref, second_ref, cotangent_ref, arrived_ref, unit_one_ref,
                  inverse_one_ref, normed_one_ref, slope_one_ref, unit_two_ref, inverse_two_ref,
                  normed_two_ref, slope_two_ref, weight_ref, edge_out_hbm, keep_ref, send_ref,
                  grad_round_ref, edge_out_ref, tall_ref, sems):
    rows = second_ref.shape[0]
    core = lax.axis_index("blk_2")
    other, other_cotangent = reversed_blocks(
        arrived_ref, (second_ref, cotangent_ref), partner_ref, rows // BLOCK
    )
    second = second_ref[...]
    summed = jnp.concatenate([second + other, other + second.astype(BF16).astype(F32)], axis=0)
    upstream = jnp.concatenate([cotangent_ref[...].astype(F32), other_cotangent], axis=0)
    inverse = inverse_norm(summed)
    unit = summed * inverse
    normed = unit.astype(BF16)
    preact = dot(normed, weight_ref[2])
    sigma = sigmoid(preact)
    edge_out_ref[...] = (summed[:rows] + preact[:rows] * sigma[:rows]).astype(BF16)
    copy = pltpu.make_async_copy(edge_out_ref, edge_out_hbm, sems.at[0])
    copy.start()
    grad_summed, grad_pre_three = layer_backward(
        unit, inverse, silu_slope(preact, sigma), weight_ref[2], upstream
    )
    grad_second = grad_summed[:rows] + grad_summed[rows:].astype(BF16).astype(F32)
    grad_first, grad_pre_two = layer_backward(
        unit_two_ref[...], inverse_two_ref[...], slope_two_ref[...], weight_ref[1], grad_second
    )
    grad_mixed, grad_pre_one = layer_backward(
        unit_one_ref[...], inverse_one_ref[...], slope_one_ref[...], weight_ref[0], grad_first
    )
    grad_round_ref[...] = grad_mixed.astype(BF16)
    pairs = (
        (normed_one_ref[...], grad_pre_one),
        (normed_two_ref[...], grad_pre_two),
        (normed[:rows], grad_pre_three[:rows]),
    )
    for layer, (normed, grad_pre) in enumerate(pairs):
        split_by_core(
            dot_tn(normed, grad_pre), tall_ref, keep_ref.at[layer], send_ref.at[layer], core
        )
    copy.wait()


def finish_body(grad_round_ref, blocks_ref, grad_state_hbm, token_ref, grad_state_ref, sems):
    for n in range(grad_round_ref.shape[0] // BLOCK):
        rows = slice(n * BLOCK, (n + 1) * BLOCK)
        grad_state_ref[rows, :] = dot_tn(blocks_ref[rows, :], grad_round_ref[rows, :]).astype(BF16)
    copy = pltpu.make_async_copy(grad_state_ref, grad_state_hbm, sems.at[0])
    copy.start()
    token_ref[...] = jnp.zeros_like(token_ref)
    copy.wait()


def join_body(keep_ref, other_ref, token_ref, pair_ref):
    groups, _, part = pair_ref.shape[:3]
    height = keep_ref.shape[2]
    for layer in range(3):
        for i in range(2):
            rows = (keep_ref[layer, i].astype(F32) + other_ref[layer, i].astype(F32)).astype(BF16)
            done = 0
            while done < height:
                number = height * layer + done
                g, at = number // part, number % part
                size = min(height - done, part - at)
                pair_ref[g, i, at : at + size, :] = rows[done : done + size]
                done += size


def line_body(arrived_ref, line_ref, tall_ref, wide_ref):
    high, width = line_ref.shape[0], line_ref.shape[2]
    deep = line_ref.shape[1] // 2
    total = arrived_ref[0].astype(F32)
    for g in range(1, arrived_ref.shape[0]):
        total = total + arrived_ref[g].astype(F32)
    tiles, lanes = tall_ref.shape[0], tall_ref.shape[-1]
    for t in range(tiles):
        across = slice(t * lanes, (t + 1) * lanes)
        tall_ref[t] = total[:, :, across]
        for y in range(high):
            for i in range(2):
                wide_ref[t, y, pl.ds(i, deep, stride=2), :] = tall_ref[
                    t, i, pl.ds(y, deep, stride=high), :
                ]
        line_ref[:, :, across] = wide_ref[t].astype(BF16)


def plane_body(column_ref, plane_ref):
    total = column_ref[0].astype(F32)
    for y in range(1, column_ref.shape[0]):
        total = total + column_ref[y].astype(F32)
    deep, pair = plane_ref.shape[:2]
    for z in range(deep):
        plane_ref[z] = total[pair * z : pair * (z + 1)].astype(BF16)


def near(array):
    return pltpu.with_memory_space_constraint(array, pltpu.VMEM)


def away(array):
    return pltpu.with_memory_space_constraint(array, pltpu.HBM)


def call(body, name, scalars, far, arrays, far_outs, outs, scratch):
    smem = pl.BlockSpec(memory_space=pltpu.SMEM)
    vmem = pl.BlockSpec(memory_space=pltpu.VMEM)
    anywhere = pl.BlockSpec(memory_space=pltpu.HBM)
    return pl.pallas_call(
        body,
        name=name,
        in_specs=[smem] * len(scalars) + [anywhere] * len(far) + [vmem] * len(arrays),
        out_specs=[anywhere] * len(far_outs) + [vmem] * len(outs),
        out_shape=[jax.ShapeDtypeStruct(*o) for o in far_outs] + [pltpu.VMEM(*o) for o in outs],
        scratch_shapes=scratch,
        compiler_params=pltpu.CompilerParams(vmem_limit_bytes=24 * 1024 * 1024),
    )(*scalars, *[away(array) for array in far], *[near(array) for array in arrays])


def summed_over(pieces, axis):
    arrived = lax.all_to_all(pieces, axis, split_axis=0, concat_axis=0, tiled=True)
    return arrived.astype(F32).sum(axis=0)


def local(edge_state, basis, weights, partner, cotangent):
    rows, width = edge_state.shape
    groups, deep, high, cores = (lax.axis_size(a) for a in GRP_BLK)
    total_edges = rows * groups * deep * high * cores
    turned = basis.transpose(1, 2, 0).reshape(NBR * NBR, rows // NBR)
    full = ((rows, width), F32)
    half = ((rows, width), BF16)
    slots = ((groups, 2 * BLOCK, width), BF16)
    thin = ((rows, 1), F32)
    *saved, second, sent, blocks, weights_near, partner_near, cotangent_near = call(
        forward_body, "forward", [], [partner, edge_state, turned, weights, cotangent],
        [], [],
        [full, thin, half, full, full, thin, half, full, full, slots, ((rows, BLOCK), BF16),
         (weights.shape, BF16), (partner.shape, jnp.int32), half],
        [pltpu.VMEM(*half), pltpu.VMEM(turned.shape, BF16), pltpu.VMEM(*half),
         pltpu.SMEM(partner.shape, jnp.int32), pltpu.SemaphoreType.DMA((8,))],
    )
    arrived = lax.all_to_all(sent, "grp", split_axis=0, concat_axis=0, tiled=True)
    swap = [(0, 1), (1, 0)]
    side = (3, 2, width // (2 * cores), width)
    edge_out, keep, send, grad_round = call(
        backward_body, "backward", [near(partner_near)], [],
        [second, cotangent_near, arrived, *saved, weights_near],
        [half], [(side, BF16), (side, BF16), half],
        [pltpu.VMEM(*half), pltpu.VMEM((width // 128, width, 128), F32),
         pltpu.SemaphoreType.DMA((1,))],
    )
    other = lax.ppermute(send, "blk_2", swap)
    grad_state, token = call(
        finish_body, "finish", [], [], [grad_round, blocks], [half], [((8, 128), F32)],
        [pltpu.VMEM(*half), pltpu.SemaphoreType.DMA((1,))],
    )
    part = 3 * width // (groups * cores)
    (pair,) = call(
        join_body, "join", [], [], [keep, other, token], [], [((groups, 2, part // 2, width), BF16)], [],
    )
    across = lax.all_to_all(pair, "grp", split_axis=0, concat_axis=0, tiled=True)
    (line,) = call(
        line_body, "line", [], [], [across], [], [((high, part // high, width), BF16)],
        [pltpu.VMEM((width // 128, 2, part // 2, 128), F32),
         pltpu.VMEM((width // 128, high, part // high, 128), F32)],
    )
    column = lax.all_to_all(
        line, "blk_1", split_axis=0, concat_axis=0, tiled=True
    )
    (plane,) = call(
        plane_body, "plane", [], [], [column], [],
        [((deep, part // high // deep, width), BF16)], [],
    )
    final = summed_over(plane, "blk_0")
    return edge_out, grad_state, final * (1.0 / math.sqrt(total_edges))


def solution(mesh):
    split = Mesh(mesh.devices.reshape(mesh.shape["grp"], 12, 8, 2), GRP_BLK)
    return jax.shard_map(
        local,
        mesh=split,
        in_specs=(P(GRP_BLK, None), P(GRP_BLK, None, None), P(), P(GRP_BLK), P(GRP_BLK, None)),
        out_specs=(P(GRP_BLK, None), P(GRP_BLK, None), P(GRP_BLK, None)),
        check_vma=False,
    )
```

```python
import math

import jax
import jax.numpy as jnp
from jax import lax
from jax.experimental import pallas as pl
from jax.experimental.pallas import tpu as pltpu
from jax.sharding import Mesh
from jax.sharding import PartitionSpec as P

NBR = 16
BLOCK = 128
GRP_BLK = ("grp", "blk_0", "blk_1", "blk_2")
BF16 = jnp.bfloat16
F32 = jnp.float32


def dot(a, b):
    return jnp.dot(a, b, preferred_element_type=F32)


def dot_nt(a, b):
    return lax.dot_general(a, b, (((1,), (1,)), ((), ())), preferred_element_type=F32)


def dot_tn(a, b):
    return lax.dot_general(a, b, (((0,), (0,)), ((), ())), preferred_element_type=F32)


def inverse_norm(hidden):
    return lax.rsqrt(jnp.mean(hidden * hidden, axis=-1, keepdims=True) + 1e-06)


def sigmoid(v):
    return 0.5 + 0.5 * jnp.tanh(0.5 * v)


def silu_slope(gated, sigma):
    return sigma + gated * (1.0 - sigma)


def layer_backward(unit, inverse, slope, weight, upstream):
    grad_pre = (upstream * slope).astype(BF16)
    grad_normed = dot_nt(grad_pre, weight)
    inner = jnp.mean(grad_normed * unit, axis=-1, keepdims=True)
    return upstream + inverse * (grad_normed - unit * inner), grad_pre


def basis_choices(atoms):
    pairs = NBR * NBR
    rows = atoms * NBR
    row = lax.broadcasted_iota(jnp.int32, (rows, atoms), 0)
    col = lax.broadcasted_iota(jnp.int32, (rows, atoms), 1)
    repeat = jnp.where(row // NBR == col, 1.0, 0.0).astype(BF16)
    row = lax.broadcasted_iota(jnp.int32, (pairs, BLOCK), 0)
    col = lax.broadcasted_iota(jnp.int32, (pairs, BLOCK), 1)
    return repeat, jnp.where(row % NBR == col % NBR, 1.0, 0.0).astype(BF16)


def basis_blocks(turned, repeat, fold):
    rows = repeat.shape[0]
    pairs = turned.shape[0]
    wide = dot_nt(repeat, turned)
    row = lax.broadcasted_iota(jnp.int32, (rows, pairs), 0)
    col = lax.broadcasted_iota(jnp.int32, (rows, pairs), 1)
    wide = jnp.where(row % NBR == col // NBR, wide, 0.0).astype(BF16)
    tiled = dot(wide, fold)
    row = lax.broadcasted_iota(jnp.int32, (rows, BLOCK), 0)
    col = lax.broadcasted_iota(jnp.int32, (rows, BLOCK), 1)
    return jnp.where((row % BLOCK) // NBR == col // NBR, tiled, 0.0).astype(BF16)


def owner_of(number, count):
    owner = jnp.int32(0)
    for edge in range(1, 4):
        owner = owner + (number >= edge * count).astype(jnp.int32)
    return owner


def fill_slots(slots_ref, at, source_ref, partner_ref, count):
    owners = [owner_of(partner_ref[n], count) for n in range(count)]
    for d in range(slots_ref.shape[0]):
        pick = jnp.int32(0)
        for n in range(1, count):
            pick = jnp.where(owners[n] == d, n, pick)
        start = pl.multiple_of(pick * BLOCK, BLOCK)
        slots_ref[d, at * BLOCK : (at + 1) * BLOCK, :] = source_ref[pl.ds(start, BLOCK), :]


def reversed_blocks(arrived_ref, sources, partner_ref, count):
    row = lax.broadcasted_iota(jnp.int32, (BLOCK, BLOCK), 0)
    col = lax.broadcasted_iota(jnp.int32, (BLOCK, BLOCK), 1)
    flip = jnp.where(row + 1 - 2 * (row % 2) == col, 1.0, 0.0).astype(BF16)
    own = lax.axis_index("grp")
    picked = [[] for _ in sources]
    for n in range(count):
        number = partner_ref[n]
        owner = owner_of(number, count)
        start = pl.multiple_of((number - owner * count) * BLOCK, BLOCK)
        for at, source_ref in enumerate(sources):
            near = source_ref[pl.ds(start, BLOCK), :].astype(BF16)
            far = arrived_ref[owner, at * BLOCK : (at + 1) * BLOCK, :]
            picked[at].append(dot(flip, jnp.where(owner == own, near, far)))
    return [jnp.concatenate(blocks, axis=0) for blocks in picked]


def forward_body(partner_hbm, edge_hbm, turned_hbm, weight_hbm, cotangent_hbm, unit_one_ref, inverse_one_ref,
                 normed_one_ref, slope_one_ref, unit_two_ref, inverse_two_ref, normed_two_ref,
                 slope_two_ref, second_ref, slots_ref, blocks_ref, weight_ref, partner_near_ref,
                 cotangent_ref,
                 edge_ref, turned_ref, sent_ref, partner_ref, sems):
    rows = edge_ref.shape[0]
    count = rows // BLOCK
    turned_copy = pltpu.make_async_copy(turned_hbm, turned_ref, sems.at[0])
    edge_copy = pltpu.make_async_copy(edge_hbm, edge_ref, sems.at[1])
    weight_copies = [
        pltpu.make_async_copy(weight_hbm.at[n], weight_ref.at[n], sems.at[2 + n]) for n in range(3)
    ]
    partner_copies = [
        pltpu.make_async_copy(partner_hbm, partner_ref, sems.at[5]),
        pltpu.make_async_copy(partner_hbm, partner_near_ref, sems.at[6]),
        pltpu.make_async_copy(cotangent_hbm, cotangent_ref, sems.at[7]),
    ]
    turned_copy.start()
    edge_copy.start()
    for copy in weight_copies + partner_copies:
        copy.start()
    repeat, fold = basis_choices(rows // NBR)
    turned_copy.wait()
    blocks_ref[...] = basis_blocks(turned_ref[...], repeat, fold)
    edge_copy.wait()
    mixed = jnp.concatenate(
        [
            dot(blocks_ref[n * BLOCK : (n + 1) * BLOCK, :], edge_ref[n * BLOCK : (n + 1) * BLOCK, :])
            for n in range(count)
        ],
        axis=0,
    )
    inverse = inverse_norm(mixed)
    unit = mixed * inverse
    normed = unit.astype(BF16)
    unit_one_ref[...] = unit
    inverse_one_ref[...] = inverse
    normed_one_ref[...] = normed
    weight_copies[0].wait()
    preact = dot(normed, weight_ref[0])
    sigma = sigmoid(preact)
    gated = preact * sigma
    slope_one_ref[...] = silu_slope(gated, sigma)
    first = mixed + gated
    inverse = inverse_norm(first)
    unit = first * inverse
    normed = unit.astype(BF16)
    unit_two_ref[...] = unit
    inverse_two_ref[...] = inverse
    normed_two_ref[...] = normed
    for copy in [weight_copies[1], *partner_copies]:
        copy.wait()
    fill_slots(slots_ref, 1, cotangent_ref, partner_ref, count)
    preact = dot(normed, weight_ref[1])
    sigma = sigmoid(preact)
    gated = preact * sigma
    slope_two_ref[...] = silu_slope(gated, sigma)
    second = first + gated
    second_ref[...] = second
    sent_ref[...] = second.astype(BF16)
    fill_slots(slots_ref, 0, sent_ref, partner_ref, count)
    weight_copies[2].wait()


def split_by_core(grad_weight, tall_ref, keep_ref, send_ref, core):
    tiles, height, lanes = tall_ref.shape
    for t in range(tiles):
        tall_ref[t] = grad_weight[:, t * lanes : (t + 1) * lanes]
    for to_ref, side in ((keep_ref, core), (send_ref, 1 - core)):
        for i in range(2):
            for t in range(tiles):
                rows = tall_ref[t, pl.ds(2 * side + i, height // 4, stride=4), :]
                to_ref[i, :, t * lanes : (t + 1) * lanes] = rows.astype(BF16)


def backward_body(partner_ref, second_ref, cotangent_ref, arrived_ref, unit_one_ref,
                  inverse_one_ref, normed_one_ref, slope_one_ref, unit_two_ref, inverse_two_ref,
                  normed_two_ref, slope_two_ref, weight_ref, edge_out_hbm, keep_ref, send_ref,
                  grad_round_ref, edge_out_ref, tall_ref, sems):
    rows = second_ref.shape[0]
    core = lax.axis_index("blk_2")
    other, other_cotangent = reversed_blocks(
        arrived_ref, (second_ref, cotangent_ref), partner_ref, rows // BLOCK
    )
    second = second_ref[...]
    summed = jnp.concatenate([second + other, other + second.astype(BF16).astype(F32)], axis=0)
    upstream = jnp.concatenate([cotangent_ref[...].astype(F32), other_cotangent], axis=0)
    inverse = inverse_norm(summed)
    unit = summed * inverse
    normed = unit.astype(BF16)
    preact = dot(normed, weight_ref[2])
    sigma = sigmoid(preact)
    gated = preact * sigma
    edge_out_ref[...] = (summed[:rows] + gated[:rows]).astype(BF16)
    copy = pltpu.make_async_copy(edge_out_ref, edge_out_hbm, sems.at[0])
    copy.start()
    grad_summed, grad_pre_three = layer_backward(
        unit, inverse, silu_slope(gated, sigma), weight_ref[2], upstream
    )
    grad_second = grad_summed[:rows] + grad_summed[rows:].astype(BF16).astype(F32)
    grad_first, grad_pre_two = layer_backward(
        unit_two_ref[...], inverse_two_ref[...], slope_two_ref[...], weight_ref[1], grad_second
    )
    grad_mixed, grad_pre_one = layer_backward(
        unit_one_ref[...], inverse_one_ref[...], slope_one_ref[...], weight_ref[0], grad_first
    )
    grad_round_ref[...] = grad_mixed.astype(BF16)
    pairs = (
        (normed_one_ref[...], grad_pre_one),
        (normed_two_ref[...], grad_pre_two),
        (normed[:rows], grad_pre_three[:rows]),
    )
    for layer, (normed, grad_pre) in enumerate(pairs):
        split_by_core(
            dot_tn(normed, grad_pre), tall_ref, keep_ref.at[layer], send_ref.at[layer], core
        )
    copy.wait()


def finish_body(grad_round_ref, blocks_ref, grad_state_hbm, token_ref, grad_state_ref, sems):
    for n in range(grad_round_ref.shape[0] // BLOCK):
        rows = slice(n * BLOCK, (n + 1) * BLOCK)
        grad_state_ref[rows, :] = dot_tn(blocks_ref[rows, :], grad_round_ref[rows, :]).astype(BF16)
    copy = pltpu.make_async_copy(grad_state_ref, grad_state_hbm, sems.at[0])
    copy.start()
    token_ref[...] = jnp.zeros_like(token_ref)
    copy.wait()


def join_body(keep_ref, other_ref, token_ref, pair_ref):
    groups, _, part = pair_ref.shape[:3]
    height = keep_ref.shape[2]
    for layer in range(3):
        for i in range(2):
            rows = (keep_ref[layer, i].astype(F32) + other_ref[layer, i].astype(F32)).astype(BF16)
            done = 0
            while done < height:
                number = height * layer + done
                g, at = number // part, number % part
                size = min(height - done, part - at)
                pair_ref[g, i, at : at + size, :] = rows[done : done + size]
                done += size


def line_body(arrived_ref, line_ref, tall_ref, wide_ref):
    high, width = line_ref.shape[0], line_ref.shape[2]
    deep = line_ref.shape[1] // 2
    total = arrived_ref[0].astype(F32)
    for g in range(1, arrived_ref.shape[0]):
        total = total + arrived_ref[g].astype(F32)
    tiles, lanes = tall_ref.shape[0], tall_ref.shape[-1]
    for t in range(tiles):
        across = slice(t * lanes, (t + 1) * lanes)
        tall_ref[t] = total[:, :, across]
        for y in range(high):
            for i in range(2):
                wide_ref[t, y, pl.ds(i, deep, stride=2), :] = tall_ref[
                    t, i, pl.ds(y, deep, stride=high), :
                ]
        line_ref[:, :, across] = wide_ref[t].astype(BF16)


def plane_body(column_ref, plane_ref):
    total = column_ref[0].astype(F32)
    for y in range(1, column_ref.shape[0]):
        total = total + column_ref[y].astype(F32)
    deep, pair = plane_ref.shape[:2]
    for z in range(deep):
        plane_ref[z] = total[pair * z : pair * (z + 1)].astype(BF16)


def near(array):
    return pltpu.with_memory_space_constraint(array, pltpu.VMEM)


def away(array):
    return pltpu.with_memory_space_constraint(array, pltpu.HBM)


def call(body, name, scalars, far, arrays, far_outs, outs, scratch):
    smem = pl.BlockSpec(memory_space=pltpu.SMEM)
    vmem = pl.BlockSpec(memory_space=pltpu.VMEM)
    anywhere = pl.BlockSpec(memory_space=pltpu.HBM)
    return pl.pallas_call(
        body,
        name=name,
        in_specs=[smem] * len(scalars) + [anywhere] * len(far) + [vmem] * len(arrays),
        out_specs=[anywhere] * len(far_outs) + [vmem] * len(outs),
        out_shape=[jax.ShapeDtypeStruct(*o) for o in far_outs] + [pltpu.VMEM(*o) for o in outs],
        scratch_shapes=scratch,
        compiler_params=pltpu.CompilerParams(vmem_limit_bytes=24 * 1024 * 1024),
    )(*scalars, *[away(array) for array in far], *[near(array) for array in arrays])


def summed_over(pieces, axis):
    arrived = lax.all_to_all(pieces, axis, split_axis=0, concat_axis=0, tiled=True)
    return arrived.astype(F32).sum(axis=0)


def local(edge_state, basis, weights, partner, cotangent):
    rows, width = edge_state.shape
    groups, deep, high, cores = (lax.axis_size(a) for a in GRP_BLK)
    total_edges = rows * groups * deep * high * cores
    turned = basis.transpose(1, 2, 0).reshape(NBR * NBR, rows // NBR)
    full = ((rows, width), F32)
    half = ((rows, width), BF16)
    slots = ((groups, 2 * BLOCK, width), BF16)
    thin = ((rows, 1), F32)
    *saved, second, sent, blocks, weights_near, partner_near, cotangent_near = call(
        forward_body, "forward", [], [partner, edge_state, turned, weights, cotangent],
        [], [],
        [full, thin, half, full, full, thin, half, full, full, slots, ((rows, BLOCK), BF16),
         (weights.shape, BF16), (partner.shape, jnp.int32), half],
        [pltpu.VMEM(*half), pltpu.VMEM(turned.shape, BF16), pltpu.VMEM(*half),
         pltpu.SMEM(partner.shape, jnp.int32), pltpu.SemaphoreType.DMA((8,))],
    )
    arrived = lax.all_to_all(sent, "grp", split_axis=0, concat_axis=0, tiled=True)
    swap = [(0, 1), (1, 0)]
    side = (3, 2, width // (2 * cores), width)
    edge_out, keep, send, grad_round = call(
        backward_body, "backward", [near(partner_near)], [],
        [second, cotangent_near, arrived, *saved, weights_near],
        [half], [(side, BF16), (side, BF16), half],
        [pltpu.VMEM(*half), pltpu.VMEM((width // 128, width, 128), F32),
         pltpu.SemaphoreType.DMA((1,))],
    )
    other = lax.ppermute(send, "blk_2", swap)
    grad_state, token = call(
        finish_body, "finish", [], [], [grad_round, blocks], [half], [((8, 128), F32)],
        [pltpu.VMEM(*half), pltpu.SemaphoreType.DMA((1,))],
    )
    part = 3 * width // (groups * cores)
    (pair,) = call(
        join_body, "join", [], [], [keep, other, token], [], [((groups, 2, part // 2, width), BF16)], [],
    )
    across = lax.all_to_all(pair, "grp", split_axis=0, concat_axis=0, tiled=True)
    (line,) = call(
        line_body, "line", [], [], [across], [], [((high, part // high, width), BF16)],
        [pltpu.VMEM((width // 128, 2, part // 2, 128), F32),
         pltpu.VMEM((width // 128, high, part // high, 128), F32)],
    )
    column = lax.all_to_all(
        line, "blk_1", split_axis=0, concat_axis=0, tiled=True
    )
    (plane,) = call(
        plane_body, "plane", [], [], [column], [],
        [((deep, part // high // deep, width), BF16)], [],
    )
    final = summed_over(plane, "blk_0")
    return edge_out, grad_state, final * (1.0 / math.sqrt(total_edges))


def solution(mesh):
    split = Mesh(mesh.devices.reshape(mesh.shape["grp"], 12, 8, 2), GRP_BLK)
    return jax.shard_map(
        local,
        mesh=split,
        in_specs=(P(GRP_BLK, None), P(GRP_BLK, None, None), P(), P(GRP_BLK), P(GRP_BLK, None)),
        out_specs=(P(GRP_BLK, None), P(GRP_BLK, None), P(GRP_BLK, None)),
        check_vma=False,
    )
```
